32 devices in a mesh: dp: 2 (over core), ctx: 4 (over z), vocab: 4 (over y, x).
Axes of the slice: x: 2, y: 2, z: 4, core: 2. Of those that a mesh axis runs over, the one named last changes fastest.
Arguments:
- hidden: bfloat16 [512, 4096], P(('dp', 'ctx')), may hold values from -32 to 32
- head_weight: bfloat16 [4096, 9504], P(None, ('ctx', 'vocab')), may hold values from -2 to 2
- targets: int32 [512], P('dp'), may hold values from 0 to 9503
- segment_ids: int32 [512], P('dp'), may hold values from 0 to 31, as said below
- lengths: int32 [32], replicated, may hold values from 8 to 24, as said below
- loss_mask: int32 [512], P('dp'), may hold values 0 or 1
- advantages: float32 [32], replicated, may hold values from -4 to 4
- ref_logprobs: float32 [512], P('dp'), may hold values from -40 to -2
Outputs:
- grad_hidden: bfloat16 [512, 4096], P(('dp', 'ctx', 'vocab'))
- grad_head: bfloat16 [4096, 9504], P(None, ('ctx', 'vocab'))
The draws below stay inside these ranges and needn't reach their ends.
Inputs may be any that keep to these rules, and one draw needn't show every extreme that they name: `segment_ids`: each sequence's tokens are contiguous; the tokens b * 64 to (b + 1) * 64 - 1 carry ids b * 4 to (b + 1) * 4 - 1, never falling, each id used. lengths[s] is the number of tokens whose segment id is s.
All inputs are finite; a program needn't handle non-finite values. No bound on the sum of `loss_mask` on one device may be relied on, other than what follows from the above.
Results may differ from the reference program's by a relative error of at most 0.012.
Values may be sent and summed in bfloat16 or wider, within the bound.
A program may use at most 128 MiB of HBM per device.

```python
import math
import jax
import jax.numpy as jnp
import numpy as np
from jax import lax

D = 4096
V_DEV = 594
TOK_DEV = 64
SEQ_DEV = 4
LOSS_SCALE = 1024
V = 9504
TOK_GRP = 256
TOKENS = 512
N_SEQ = 32
N_DP = 2
N_CTX = 4
N_VOCAB = 4


def plan_lengths(key):
    block_total = N_DP * N_CTX
    base_length = TOK_DEV // (2 * SEQ_DEV)
    spare_tokens = TOK_DEV - SEQ_DEV * base_length
    big_extra = (spare_tokens + 1) // 2
    rest_tokens = spare_tokens - big_extra
    cut_points = jnp.sort(jax.random.randint(jax.random.fold_in(key, 11), (block_total, SEQ_DEV - 2), 0, rest_tokens + 1), axis=1)
    boundaries = jnp.concatenate([jnp.zeros((block_total, 1), jnp.int32), cut_points.astype(jnp.int32), jnp.full((block_total, 1), rest_tokens, jnp.int32)], axis=1)
    others = base_length + boundaries[:, 1:] - boundaries[:, :-1]
    big_place = jax.random.randint(jax.random.fold_in(key, 13), (block_total, 1), 0, SEQ_DEV)
    slot = jnp.arange(SEQ_DEV, dtype=jnp.int32)[None, :]
    other_index = jnp.clip(slot - (slot > big_place).astype(jnp.int32), 0, SEQ_DEV - 2)
    picked = jnp.take_along_axis(others, other_index, axis=1)
    return jnp.where(slot == big_place, base_length + big_extra, picked).astype(jnp.int32)


def draw_lengths(key, part):
    return plan_lengths(key).reshape(-1).astype(jnp.int32)


def draw_segment_ids(key, part):
    seq_sizes = plan_lengths(key)
    seq_ends = jnp.cumsum(seq_sizes, axis=1)
    position = jnp.arange(TOK_DEV, dtype=jnp.int32)
    local_index = jnp.sum((position[None, :, None] >= seq_ends[:, None, :-1]).astype(jnp.int32), axis=2)
    offsets = SEQ_DEV * jnp.arange(N_DP * N_CTX, dtype=jnp.int32)
    return (local_index + offsets[:, None]).reshape(-1).astype(jnp.int32)


def draw_hidden(key, part):
    noise = jax.random.truncated_normal(jax.random.fold_in(key, 1), -5.0, 5.0, (TOKENS, D), jnp.float32)
    row_scales = jnp.exp(jax.random.uniform(jax.random.fold_in(key, 5), (TOKENS,), jnp.float32, jnp.log(0.3), jnp.log(3.0)))
    matrix = row_scales[:, None] * noise
    return jnp.clip(matrix, -32.0, 32.0).astype(jnp.bfloat16)


def draw_head_weight(key, part):
    noise = jax.random.truncated_normal(jax.random.fold_in(key, 2), -5.0, 5.0, (D, V), jnp.float32) / jnp.sqrt(float(D))
    position = jnp.arange(V, dtype=jnp.float32) / V
    spread = jnp.exp(jax.random.uniform(jax.random.fold_in(key, 4), (V,), jnp.float32, 0.0, jnp.log(10.0)))
    column_scales = 0.25 * spread * jnp.exp(jnp.log(3.0) * position)
    matrix = noise * column_scales[None, :]
    return jnp.clip(matrix, -2.0, 2.0).astype(jnp.bfloat16)


def set_ends(values, key, least, top_value):
    place = [jax.random.randint(jax.random.fold_in(key, axis), (), 0, length) for axis, length in enumerate(values.shape)]
    main_axis = values.shape.index(max(values.shape))
    beside = place[:main_axis] + [(place[main_axis] + 1) % values.shape[main_axis]] + place[main_axis + 1:]
    return values.at[tuple(place)].set(least).at[tuple(beside)].set(top_value)


def block_levels(own_key, shape, shards, low, top_value):
    loudness, own = 1.0, jax.random.fold_in(own_key, 6)
    for dim, shards_of in shards:
        steps = jnp.exp(jax.random.uniform(jax.random.fold_in(own, dim), (shards_of,), jnp.float32, low / len(shards), top_value / len(shards)))
        loudness = loudness * jnp.repeat(steps, shape[dim] // shards_of).reshape([-1 if axis == dim else 1 for axis in range(len(shape))])
    return loudness


def rank_table(amount, slope):
    portions = [(1 << 20) // math.isqrt(rank ** slope) + 1 for rank in range(1, amount + 1)]
    deviation = 1 + sum(portions) // (1 << 30)
    return np.cumsum(np.array([max(1, weight // deviation) for weight in portions]))


def skewed_ids(own_key, dims, count, slope):
    listing = rank_table(count, slope)
    ticket = jax.random.randint(jax.random.fold_in(own_key, 1), dims, 0, int(listing[count - 1]))
    rank = jnp.searchsorted(jnp.asarray(listing, jnp.int32), ticket, side="right")
    return jax.random.permutation(jax.random.fold_in(own_key, 2), count)[rank].astype(jnp.int32)


def bell_draw(rng, shape, scale, limit, held_as=jnp.bfloat16):
    return jnp.clip(scale * jax.random.normal(rng, shape, jnp.float32), -limit, limit).astype(held_as)


def setup_inputs(seed: int = 0) -> dict:
    streams_of = jax.random.split(jax.random.key(seed), 9)
    hidden = draw_hidden(jax.random.fold_in(streams_of[8], 71), 0)
    head_weight = draw_head_weight(jax.random.fold_in(streams_of[8], 71), 0)
    targets = set_ends(skewed_ids(streams_of[2], (TOKENS,), V, 2), jax.random.fold_in(streams_of[2], 3), 0, V - 1).astype(jnp.int32)
    segment_ids = draw_segment_ids(jax.random.fold_in(streams_of[8], 71), 0)
    lengths = draw_lengths(jax.random.fold_in(streams_of[8], 71), 0)
    loss_mask = set_ends((jax.random.randint(streams_of[5], (TOKENS,), 0, 4) < 3).astype(jnp.int32), jax.random.fold_in(streams_of[5], 1), 0, 1)
    advantages = bell_draw(streams_of[6], (N_SEQ,), 1.0, 4.0, jnp.float32)
    ref_logprobs = jnp.clip(-40.0 + 38.0 * jax.random.uniform(streams_of[7], (TOKENS,), jnp.float32) ** block_levels(streams_of[7], (TOKENS,), ((0, 2),), -0.2, 0.2), -40.0, -2.0)
    return {"hidden": hidden, "head_weight": head_weight, "targets": targets, "segment_ids": segment_ids, "lengths": lengths, "loss_mask": loss_mask, "advantages": advantages, "ref_logprobs": ref_logprobs}


kl_weight = 0.1
entropy_weight = 0.05


def combine_stats(left_stats, right_stats):
    max_one, sum_one, logit_one, target_one = left_stats
    max_two, sum_two, logit_two, target_two = right_stats
    new_max = jnp.maximum(max_one, max_two)
    scale_one = jnp.exp(max_one - new_max)
    scale_two = jnp.exp(max_two - new_max)
    return (new_max, sum_one * scale_one + sum_two * scale_two,
            logit_one * scale_one + logit_two * scale_two, target_one + target_two)


def reference(hidden, head_weight, targets, segment_ids, lengths, loss_mask, advantages, ref_logprobs):
    block_count = N_CTX * N_VOCAB
    first_columns = jnp.arange(block_count, dtype=jnp.int32) * V_DEV

    def block_logits(first_column):
        weight_block = lax.dynamic_slice_in_dim(head_weight, first_column, V_DEV, 1)
        logits = jnp.dot(hidden, weight_block, preferred_element_type=jnp.float32)
        columns = first_column + jnp.arange(V_DEV, dtype=jnp.int32)
        target_hits = targets[:, None] == columns[None, :]
        return weight_block, logits, target_hits

    def stats_step(carry, first_column):
        weight_block, logits, target_hits = block_logits(first_column)
        local_max = jnp.max(logits, axis=1)
        shifted = jnp.exp(logits - local_max[:, None])
        stats = (local_max, jnp.sum(shifted, axis=1), jnp.sum(shifted * logits, axis=1),
                 jnp.sum(jnp.where(target_hits, logits, 0.0), axis=1))
        return combine_stats(carry, stats), None

    start_stats = (jnp.full((TOKENS,), -jnp.inf, jnp.float32), jnp.zeros((TOKENS,), jnp.float32),
                   jnp.zeros((TOKENS,), jnp.float32), jnp.zeros((TOKENS,), jnp.float32))
    stats, unused = lax.scan(stats_step, start_stats, first_columns)
    row_max, exp_total, exp_logit, target_logit = stats
    log_total = row_max + jnp.log(exp_total)
    target_logp = target_logit - log_total
    mean_logit = exp_logit / exp_total

    seq_onehot = segment_ids[:, None] == jnp.arange(N_SEQ, dtype=jnp.int32)[None, :]
    token_adv = jnp.sum(jnp.where(seq_onehot, advantages[None, :], 0.0), axis=1)
    token_len = jnp.sum(jnp.where(seq_onehot, lengths[None, :].astype(jnp.float32), 0.0), axis=1)
    token_weight = LOSS_SCALE * loss_mask.astype(jnp.float32) / token_len
    logp_grad = -token_adv + kl_weight * (target_logp - ref_logprobs)
    hidden_wide = hidden.reshape(N_DP, TOK_GRP, D).astype(jnp.float32)

    def grad_step(carry, first_column):
        weight_block, logits, target_hits = block_logits(first_column)
        probs = jnp.exp(logits - log_total[:, None])
        inner = logp_grad[:, None] * (target_hits.astype(jnp.float32) - probs)
        inner = inner + entropy_weight * probs * (logits - mean_logit[:, None])
        grad_logits = (token_weight[:, None] * inner).astype(jnp.bfloat16)
        carry = carry + jnp.dot(grad_logits, weight_block.T, preferred_element_type=jnp.float32)
        halves = jnp.einsum("gtd,gtv->gdv", hidden_wide,
                            grad_logits.reshape(N_DP, TOK_GRP, V_DEV).astype(jnp.float32))
        halves = lax.optimization_barrier(halves.astype(jnp.bfloat16)).astype(jnp.float32)
        return carry, jnp.sum(halves, axis=0).astype(jnp.bfloat16)

    grad_rows, head_blocks = lax.scan(grad_step, jnp.zeros((TOKENS, D), jnp.float32), first_columns)
    grad_head = jnp.transpose(head_blocks, (1, 0, 2)).reshape(D, V)
    return grad_rows.astype(jnp.bfloat16), grad_head
```

```python
import functools

import jax
import jax.numpy as jnp
from jax import lax
from jax.experimental import pallas as pl
from jax.experimental.pallas import tpu as pltpu
from jax.sharding import PartitionSpec as P

LOSS_SCALE = 1024


kl_weight = 0.1
entropy_weight = 0.05
MESH = pl.DeviceIdType.MESH
CHUNKS = 4
STATS = 8


def combine(parts):
    top = functools.reduce(jnp.maximum, [p[0:1] for p in parts])
    scales = [jnp.exp(p[0:1] - top) for p in parts]
    total = sum(p[1:2] * s for p, s in zip(parts, scales))
    logit = sum(p[2:3] * s for p, s in zip(parts, scales))
    target = sum(p[3:4] for p in parts)
    return top, total, logit, target


def kernel(
    n_dp, n_ctx, n_vocab,
    hid, head, lengths, advantages, targets, segments, mask, ref_lp,
    rows_out, hid_all, grad_all,
    weight, hbuf, logits, rowbuf, colbuf, tcol, statcol, stat_own, stat_mid, stat_v, stat_c,
    gbuf, pbuf, part_v, sums, part_c,
    local_sem, z_send, z_recv, x_send, x_recv, d_send, d_recv, g_send, g_recv,
    sv_send, sv_recv, sc_send, sc_recv, a_send, a_recv, b_send, b_recv,
):
    g, c, v = lax.axis_index("dp"), lax.axis_index("ctx"), lax.axis_index("vocab")
    block, depth = hid.shape
    tokens, width = logits.shape
    quarter = depth // n_vocab
    chunk = depth // CHUNKS
    out_rows = rows_out.shape[0]

    def up(axis, n, step):
        return lax.rem(axis + step, n)

    def down(axis, n, step):
        return lax.rem(axis + n - step, n)

    def remote(src, dst, send, recv, where):
        copy = pltpu.make_async_remote_copy(
            src_ref=src, dst_ref=dst, send_sem=send, recv_sem=recv,
            device_id=where, device_id_type=MESH,
        )
        return copy

    load_w = pltpu.make_async_copy(head, weight, local_sem.at[0])
    load_w.start()
    own_rows = pl.ds(pl.multiple_of(c * block, block), block)
    load_h = pltpu.make_async_copy(hid, hbuf.at[own_rows], local_sem.at[1])
    load_h.start()

    barrier = pltpu.get_barrier_semaphore()
    for step in range(1, n_ctx):
        pl.semaphore_signal(barrier, inc=1, device_id=(g, up(c, n_ctx, step), v), device_id_type=MESH)
    for step in range(1, n_vocab):
        pl.semaphore_signal(barrier, inc=1, device_id=(g, c, up(v, n_vocab, step)), device_id_type=MESH)
    for step in range(1, n_dp):
        pl.semaphore_signal(barrier, inc=1, device_id=(up(g, n_dp, step), c, v), device_id_type=MESH)
    pl.semaphore_wait(barrier, n_ctx + n_vocab + n_dp - 3)

    own_cols = pl.ds(pl.multiple_of(v * quarter, quarter), quarter)
    pending = []
    z_copies = []
    for step in range(1, n_ctx):
        copy = remote(
            hid.at[:, own_cols], hbuf.at[own_rows, own_cols],
            z_send.at[step - 1], z_recv.at[step - 1], (g, up(c, n_ctx, step), v),
        )
        copy.start()
        z_copies.append(copy)
        pending.append(copy)

    seg = segments[...]
    token_adv = jnp.zeros((1, tokens), jnp.float32)
    token_len = jnp.zeros((1, tokens), jnp.float32)
    for s in range(advantages.shape[0]):
        here = seg == s
        token_adv = jnp.where(here, advantages[s], token_adv)
        token_len = jnp.where(here, lengths[s].astype(jnp.float32), token_len)
    token_weight = LOSS_SCALE * mask[...].astype(jnp.float32) / token_len
    rowbuf[...] = jnp.zeros_like(rowbuf)
    rowbuf[0:1, :] = targets[...].astype(jnp.float32)
    tcol[...] = rowbuf[...].T

    first_column = (c * n_vocab + v) * width
    columns = (first_column + lax.broadcasted_iota(jnp.int32, (block, width), 1)).astype(jnp.float32)
    lane = lax.broadcasted_iota(jnp.int32, (block, 128), 1)

    def do_block(owner):
        rows = pl.ds(pl.multiple_of(owner * block, block), block)
        x = jnp.dot(hbuf[rows, :], weight[...], preferred_element_type=jnp.float32)
        logits[rows, :] = x
        top = jnp.max(x, axis=1, keepdims=True)
        e = jnp.exp(x - top)
        total = jnp.sum(e, axis=1, keepdims=True)
        logit = jnp.sum(e * x, axis=1, keepdims=True)
        hit = tcol[rows, 0:1] == columns
        target = jnp.sum(jnp.where(hit, x, 0.0), axis=1, keepdims=True)
        statcol[rows, :] = jnp.where(
            lane == 0, top, jnp.where(lane == 1, total, jnp.where(lane == 2, logit, jnp.where(lane == 3, target, 0.0)))
        )

    load_w.wait()
    load_h.wait()
    do_block(c)

    x_copies = []
    for step in range(1, n_ctx):
        z_copies[step - 1].wait_recv()
        owner = down(c, n_ctx, step)
        rows = pl.ds(pl.multiple_of(owner * block, block), block)
        for hop in range(1, n_vocab):
            copy = remote(
                hbuf.at[rows, own_cols], hbuf.at[rows, own_cols],
                x_send.at[step - 1, hop - 1], x_recv.at[step - 1, hop - 1], (g, c, up(v, n_vocab, hop)),
            )
            copy.start()
            x_copies.append(copy)
    for step in range(1, n_ctx):
        for hop in range(1, n_vocab):
            x_copies[(step - 1) * (n_vocab - 1) + hop - 1].wait_recv()
        do_block(down(c, n_ctx, step))

    store_h = pltpu.make_async_copy(hbuf, hid_all.at[g], local_sem.at[2])
    store_h.start()
    d_copies = []
    for step in range(1, n_dp):
        copy = remote(hbuf, hid_all.at[g], d_send.at[step - 1], d_recv.at[step - 1], (up(g, n_dp, step), c, v))
        copy.start()
        d_copies.append(copy)

    stat_own[...] = statcol[...].T[0:STATS, :]
    s_copies = []
    for step in range(1, n_vocab):
        copy = remote(stat_own, stat_v.at[step - 1], sv_send.at[step - 1], sv_recv.at[step - 1], (g, c, up(v, n_vocab, step)))
        copy.start()
        s_copies.append(copy)
    for copy in s_copies:
        copy.wait_recv()
    pending += s_copies
    merged = combine([stat_own[...]] + [stat_v[i] for i in range(n_vocab - 1)])
    for i, row in enumerate(merged):
        stat_mid[i : i + 1, :] = row
    s_copies = []
    for step in range(1, n_ctx):
        copy = remote(stat_mid, stat_c.at[step - 1], sc_send.at[step - 1], sc_recv.at[step - 1], (g, up(c, n_ctx, step), v))
        copy.start()
        s_copies.append(copy)
    for copy in s_copies:
        copy.wait_recv()
    pending += s_copies
    row_max, exp_total, exp_logit, target_logit = combine([stat_mid[...]] + [stat_c[i] for i in range(n_ctx - 1)])
    log_total = row_max + jnp.log(exp_total)
    rowbuf[0:1, :] = log_total
    rowbuf[1:2, :] = exp_logit / exp_total
    rowbuf[2:3, :] = -token_adv + kl_weight * ((target_logit - log_total) - ref_lp[...])
    rowbuf[3:4, :] = token_weight
    colbuf[...] = rowbuf[...].T

    for b in range(n_ctx):
        rows = slice(b * block, (b + 1) * block)
        x = logits[rows, :]
        probs = jnp.exp(x - colbuf[rows, 0:1])
        hit = (tcol[rows, 0:1] == columns).astype(jnp.float32)
        inner = colbuf[rows, 2:3] * (hit - probs)
        inner = inner + entropy_weight * probs * (x - colbuf[rows, 1:2])
        gbuf[rows, :] = (colbuf[rows, 3:4] * inner).astype(jnp.bfloat16)

    store_g = pltpu.make_async_copy(gbuf, grad_all.at[g], local_sem.at[3])
    store_g.start()
    for step in range(1, n_dp):
        copy = remote(gbuf, grad_all.at[g], g_send.at[step - 1], g_recv.at[step - 1], (up(g, n_dp, step), c, v))
        copy.start()
        d_copies.append(copy)

    a_copies = []
    for k in range(CHUNKS):
        cols = slice(k * chunk, (k + 1) * chunk)
        part = lax.dot_general(
            gbuf[...], weight[cols, :], (((1,), (1,)), ((), ())), preferred_element_type=jnp.float32
        )
        for i in range(n_ctx):
            for j in range(n_vocab):
                first = i * block + j * out_rows
                pbuf[j, i, :, cols] = part[first : first + out_rows].astype(jnp.bfloat16)
        for step in range(1, n_vocab):
            to = up(v, n_vocab, step)
            copy = remote(
                pbuf.at[to, :, :, pl.ds(k * chunk, chunk)], part_v.at[step - 1, :, :, pl.ds(k * chunk, chunk)],
                a_send.at[k, step - 1], a_recv.at[k, step - 1], (g, c, to),
            )
            copy.start()
            a_copies.append(copy)
    b_copies = []
    for k in range(CHUNKS):
        cols = slice(k * chunk, (k + 1) * chunk)
        for step in range(1, n_vocab):
            a_copies[k * (n_vocab - 1) + step - 1].wait_recv()
        for i in range(n_ctx):
            total = pbuf[v, i, :, cols].astype(jnp.float32)
            for step in range(1, n_vocab):
                total = total + part_v[step - 1, i, :, cols].astype(jnp.float32)
            sums[i, :, cols] = total.astype(jnp.bfloat16)
        for step in range(1, n_ctx):
            to = up(c, n_ctx, step)
            copy = remote(
                sums.at[to, :, pl.ds(k * chunk, chunk)], part_c.at[step - 1, :, pl.ds(k * chunk, chunk)],
                b_send.at[k, step - 1], b_recv.at[k, step - 1], (g, to, v),
            )
            copy.start()
            b_copies.append(copy)
    for k in range(CHUNKS):
        cols = slice(k * chunk, (k + 1) * chunk)
        for step in range(1, n_ctx):
            b_copies[k * (n_ctx - 1) + step - 1].wait_recv()
        total = sums[c, :, cols].astype(jnp.float32)
        for step in range(1, n_ctx):
            total = total + part_c[step - 1, :, cols].astype(jnp.float32)
        rows_out[:, cols] = total.astype(jnp.bfloat16)

    for copy in pending + x_copies + a_copies + b_copies:
        copy.wait_send()
    for copy in d_copies:
        copy.wait()
    store_h.wait()
    store_g.wait()


def per_device(
    hidden, head_weight, targets, segment_ids, lengths, loss_mask, advantages, ref_logprobs
):
    n_dp, n_ctx, n_vocab = lax.axis_size("dp"), lax.axis_size("ctx"), lax.axis_size("vocab")
    block, depth = hidden.shape
    width = head_weight.shape[1]
    tokens = block * n_ctx
    out_rows = block // n_vocab
    bf16, f32 = jnp.bfloat16, jnp.float32
    dma = pltpu.SemaphoreType.DMA
    anywhere = pl.BlockSpec(memory_space=pl.ANY)
    smem = pl.BlockSpec(memory_space=pltpu.SMEM)
    vmem = pl.BlockSpec(memory_space=pltpu.VMEM)
    grad_hidden, hid_all, grad_all = pl.pallas_call(
        functools.partial(kernel, n_dp, n_ctx, n_vocab),
        out_shape=(
            jax.ShapeDtypeStruct((out_rows, depth), bf16),
            jax.ShapeDtypeStruct((n_dp, tokens, depth), bf16),
            jax.ShapeDtypeStruct((n_dp, tokens, width), bf16),
        ),
        in_specs=[anywhere, anywhere, smem, smem, vmem, vmem, vmem, vmem],
        out_specs=(vmem, anywhere, anywhere),
        scratch_shapes=[
            pltpu.VMEM((depth, width), bf16),
            pltpu.VMEM((tokens, depth), bf16),
            pltpu.VMEM((tokens, width), f32),
            pltpu.VMEM((128, tokens), f32),
            pltpu.VMEM((tokens, 128), f32),
            pltpu.VMEM((tokens, 128), f32),
            pltpu.VMEM((tokens, 128), f32),
            pltpu.VMEM((STATS, tokens), f32),
            pltpu.VMEM((STATS, tokens), f32),
            pltpu.VMEM((n_vocab - 1, STATS, tokens), f32),
            pltpu.VMEM((n_ctx - 1, STATS, tokens), f32),
            pltpu.VMEM((tokens, width), bf16),
            pltpu.VMEM((n_vocab, n_ctx, out_rows, depth), bf16),
            pltpu.VMEM((n_vocab - 1, n_ctx, out_rows, depth), bf16),
            pltpu.VMEM((n_ctx, out_rows, depth), bf16),
            pltpu.VMEM((n_ctx - 1, out_rows, depth), bf16),
            dma((4,)),
            dma((n_ctx - 1,)), dma((n_ctx - 1,)),
            dma((n_ctx - 1, n_vocab - 1)), dma((n_ctx - 1, n_vocab - 1)),
            dma((n_dp - 1,)), dma((n_dp - 1,)), dma((n_dp - 1,)), dma((n_dp - 1,)),
            dma((n_vocab - 1,)), dma((n_vocab - 1,)),
            dma((n_ctx - 1,)), dma((n_ctx - 1,)),
            dma((CHUNKS, n_vocab - 1)), dma((CHUNKS, n_vocab - 1)),
            dma((CHUNKS, n_ctx - 1)), dma((CHUNKS, n_ctx - 1)),
        ],
        compiler_params=pltpu.CompilerParams(collective_id=0, has_side_effects=True),
    )(
        hidden, head_weight, lengths, advantages,
        targets[None, :], segment_ids[None, :], loss_mask[None, :], ref_logprobs[None, :],
    )
    grad_head = lax.dot_general(
        hid_all.reshape(n_dp * tokens, depth),
        grad_all.reshape(n_dp * tokens, width),
        (((0,), (0,)), ((), ())),
        preferred_element_type=jnp.float32,
    ).astype(jnp.bfloat16)
    return (grad_hidden, grad_head)


def solution(mesh):
    return jax.shard_map(
        per_device,
        mesh=mesh,
        in_specs=(
            P(("dp", "ctx"), None),
            P(None, ("ctx", "vocab")),
            P("dp"),
            P("dp"),
            P(),
            P("dp"),
            P(),
            P("dp"),
        ),
        out_specs=(P(("dp", "ctx", "vocab"), None), P(None, ("ctx", "vocab"))),
        check_vma=False,
    )
```

```python
import functools
import math

import jax
import jax.numpy as jnp
from jax import lax
from jax.experimental import pallas as pl
from jax.experimental.pallas import tpu as pltpu
from jax.sharding import PartitionSpec as P

LOSS_SCALE = 1024


kl_weight = 0.1
entropy_weight = 0.05
MESH = pl.DeviceIdType.MESH
CHUNKS = 8
STATS = 8


def combine(parts):
    top = functools.reduce(jnp.maximum, [p[0:1] for p in parts])
    scales = [jnp.exp(p[0:1] - top) for p in parts]
    total = sum(p[1:2] * s for p, s in zip(parts, scales))
    logit = sum(p[2:3] * s for p, s in zip(parts, scales))
    target = sum(p[3:4] for p in parts)
    return top, total, logit, target


def kernel(
    n_dp, n_ctx, n_hi, n_lo,
    hid, head, lengths, advantages, targets, segments, mask, ref_lp,
    rows_out, hid_all, grad_all,
    weight, hbuf, logits, rowbuf, colbuf, tcol, statcol, stat_own, stat_mid, stat_v, stat_c,
    gbuf, pbuf, part_one, sum_one, part_two, sums, part_c,
    local_sem, z_send, z_recv, lo_send, lo_recv, hi_send, hi_recv, ra_send, ra_recv, rb_send, rb_recv,
    d_send, d_recv, g_send, g_recv,
    sv_send, sv_recv, sc_send, sc_recv, one_send, one_recv, two_send, two_recv, b_send, b_recv,
):
    g, c, v = lax.axis_index("dp"), lax.axis_index("ctx"), lax.axis_index("vocab")
    n_vocab = n_hi * n_lo
    hi, lo = v // n_lo, lax.rem(v, n_lo)
    block, depth = hid.shape
    tokens, width = logits.shape
    quarter = depth // n_vocab
    chunk = depth // CHUNKS
    out_rows = rows_out.shape[0]

    def up(axis, n, step):
        return lax.rem(axis + step, n)

    def down(axis, n, step):
        return lax.rem(axis + n - step, n)

    def remote(src, dst, send, recv, where):
        copy = pltpu.make_async_remote_copy(
            src_ref=src, dst_ref=dst, send_sem=send, recv_sem=recv,
            device_id=where, device_id_type=MESH,
        )
        return copy

    load_w = pltpu.make_async_copy(head, weight, local_sem.at[0])
    load_w.start()
    own_rows = pl.ds(pl.multiple_of(c * block, block), block)
    load_h = pltpu.make_async_copy(hid, hbuf.at[own_rows], local_sem.at[1])
    load_h.start()

    barrier = pltpu.get_barrier_semaphore()
    for step in range(1, n_ctx):
        pl.semaphore_signal(barrier, inc=1, device_id=(g, up(c, n_ctx, step), v), device_id_type=MESH)
    for step in range(1, n_vocab):
        pl.semaphore_signal(barrier, inc=1, device_id=(g, c, up(v, n_vocab, step)), device_id_type=MESH)
    for step in range(1, n_dp):
        pl.semaphore_signal(barrier, inc=1, device_id=(up(g, n_dp, step), c, v), device_id_type=MESH)
    pl.semaphore_wait(barrier, n_ctx + n_vocab + n_dp - 3)

    own_cols = pl.ds(pl.multiple_of(v * quarter, quarter), quarter)
    pending = []
    z_copies = []
    for step in range(1, n_ctx):
        copy = remote(
            hid.at[:, own_cols], hbuf.at[own_rows, own_cols],
            z_send.at[step - 1], z_recv.at[step - 1], (g, up(c, n_ctx, step), v),
        )
        copy.start()
        z_copies.append(copy)
        pending.append(copy)

    seg = segments[...]
    token_adv = jnp.zeros((1, tokens), jnp.float32)
    token_len = jnp.zeros((1, tokens), jnp.float32)
    for s in range(advantages.shape[0]):
        here = seg == s
        token_adv = jnp.where(here, advantages[s], token_adv)
        token_len = jnp.where(here, lengths[s].astype(jnp.float32), token_len)
    token_weight = LOSS_SCALE * mask[...].astype(jnp.float32) / token_len
    rowbuf[...] = jnp.zeros_like(rowbuf)
    rowbuf[0:1, :] = targets[...].astype(jnp.float32)
    tcol[...] = rowbuf[...].T

    first_column = (c * n_vocab + v) * width
    columns = (first_column + lax.broadcasted_iota(jnp.int32, (block, width), 1)).astype(jnp.float32)
    lane = lax.broadcasted_iota(jnp.int32, (block, 128), 1)

    def do_block(owner):
        rows = pl.ds(pl.multiple_of(owner * block, block), block)
        x = lax.dot_general(
            weight[...], hbuf[rows, :], (((1,), (1,)), ((), ())), preferred_element_type=jnp.float32
        ).T
        logits[rows, :] = x
        top = jnp.max(x, axis=1, keepdims=True)
        e = jnp.exp(x - top)
        total = jnp.sum(e, axis=1, keepdims=True)
        logit = jnp.sum(e * x, axis=1, keepdims=True)
        hit = tcol[rows, 0:1] == columns
        target = jnp.sum(jnp.where(hit, x, 0.0), axis=1, keepdims=True)
        statcol[rows, :] = jnp.where(
            lane == 0, top, jnp.where(lane == 1, total, jnp.where(lane == 2, logit, jnp.where(lane == 3, target, 0.0)))
        )

    load_w.wait()
    load_h.wait()
    do_block(c)

    half = quarter // 2

    def share(owner, column_owner, part):
        rows = pl.ds(pl.multiple_of(owner * block, block), block)
        return hbuf.at[rows, pl.ds(pl.multiple_of(column_owner * quarter + part * half, half), half)]

    def at_lo(step):
        return (g, c, hi * n_lo + up(lo, n_lo, step))

    def at_hi(step):
        return (g, c, up(hi, n_hi, step) * n_lo + lo)

    def move(ref, send, recv, where):
        copy = remote(ref, ref, send, recv, where)
        copy.start()
        pending.append(copy)
        return copy

    lo_copies, hi_copies, relays = {}, {}, {}

    def relay(step):
        owner = down(c, n_ctx, step)
        for hop in range(1, n_lo):
            lo_copies[step - 1, hop - 1, 0].wait_recv()
            source = hi * n_lo + down(lo, n_lo, hop)
            for far in range(1, n_hi):
                at = (step - 1, hop - 1, far - 1)
                relays[(step, 0) + at] = move(share(owner, source, 0), ra_send.at[at], ra_recv.at[at], at_hi(far))
        for hop in range(1, n_hi):
            hi_copies[step - 1, hop - 1, 1].wait_recv()
            source = down(hi, n_hi, hop) * n_lo + lo
            for far in range(1, n_lo):
                at = (step - 1, hop - 1, far - 1)
                relays[(step, 1) + at] = move(share(owner, source, 1), rb_send.at[at], rb_recv.at[at], at_lo(far))

    for step in range(1, n_ctx):
        z_copies[step - 1].wait_recv()
        owner = down(c, n_ctx, step)
        for part in range(2):
            for hop in range(1, n_lo):
                at = (step - 1, hop - 1, part)
                lo_copies[at] = move(share(owner, v, part), lo_send.at[at], lo_recv.at[at], at_lo(hop))
            for hop in range(1, n_hi):
                at = (step - 1, hop - 1, 1 - part)
                hi_copies[at] = move(share(owner, v, 1 - part), hi_send.at[at], hi_recv.at[at], at_hi(hop))
        if step >= 2:
            relay(step - 1)
    relay(n_ctx - 1)
    for step in range(1, n_ctx):
        for copies in (lo_copies, hi_copies):
            for at, copy in copies.items():
                if at[0] == step - 1 and at[2] == (1 if copies is lo_copies else 0):
                    copy.wait_recv()
        for at, copy in relays.items():
            if at[0] == step:
                copy.wait_recv()
        do_block(down(c, n_ctx, step))

    store_h = pltpu.make_async_copy(hbuf, hid_all.at[g], local_sem.at[2])
    store_h.start()
    d_copies = []
    for step in range(1, n_dp):
        copy = remote(hbuf, hid_all.at[g], d_send.at[step - 1], d_recv.at[step - 1], (up(g, n_dp, step), c, v))
        copy.start()
        d_copies.append(copy)

    stat_own[...] = statcol[...].T[0:STATS, :]
    s_copies = []
    for step in range(1, n_vocab):
        copy = remote(stat_own, stat_v.at[step - 1], sv_send.at[step - 1], sv_recv.at[step - 1], (g, c, up(v, n_vocab, step)))
        copy.start()
        s_copies.append(copy)
    for copy in s_copies:
        copy.wait_recv()
    pending += s_copies
    merged = combine([stat_own[...]] + [stat_v[i] for i in range(n_vocab - 1)])
    for i, row in enumerate(merged):
        stat_mid[i : i + 1, :] = row
    s_copies = []
    for step in range(1, n_ctx):
        copy = remote(stat_mid, stat_c.at[step - 1], sc_send.at[step - 1], sc_recv.at[step - 1], (g, up(c, n_ctx, step), v))
        copy.start()
        s_copies.append(copy)
    for copy in s_copies:
        copy.wait_recv()
    pending += s_copies
    row_max, exp_total, exp_logit, target_logit = combine([stat_mid[...]] + [stat_c[i] for i in range(n_ctx - 1)])
    log_total = row_max + jnp.log(exp_total)
    rowbuf[0:1, :] = log_total
    rowbuf[1:2, :] = exp_logit / exp_total
    rowbuf[2:3, :] = -token_adv + kl_weight * ((target_logit - log_total) - ref_lp[...])
    rowbuf[3:4, :] = token_weight
    colbuf[...] = rowbuf[...].T

    for b in range(n_ctx):
        rows = slice(b * block, (b + 1) * block)
        x = logits[rows, :]
        probs = jnp.exp(x - colbuf[rows, 0:1])
        hit = (tcol[rows, 0:1] == columns).astype(jnp.float32)
        inner = colbuf[rows, 2:3] * (hit - probs)
        inner = inner + entropy_weight * probs * (x - colbuf[rows, 1:2])
        gbuf[rows, :] = (colbuf[rows, 3:4] * inner).astype(jnp.bfloat16)

    store_g = pltpu.make_async_copy(gbuf, grad_all.at[g], local_sem.at[3])
    store_g.start()
    for step in range(1, n_dp):
        copy = remote(gbuf, grad_all.at[g], g_send.at[step - 1], g_recv.at[step - 1], (up(g, n_dp, step), c, v))
        copy.start()
        d_copies.append(copy)

    def span(k):
        return pl.ds(k * chunk, chunk)

    def partials(k):
        part = jnp.dot(gbuf[...], weight[:, k * chunk : (k + 1) * chunk], preferred_element_type=jnp.float32)
        for i in range(n_ctx):
            for j in range(n_vocab):
                first = i * block + j * out_rows
                pbuf[j // n_lo, j % n_lo, i, :, span(k)] = part[first : first + out_rows].astype(jnp.bfloat16)

    def stage_one(k):
        copies = []
        for step in range(1, n_hi if k % 2 else n_lo):
            if k % 2:
                source = pbuf.at[up(hi, n_hi, step), :, :, :, span(k)]
            else:
                source = pbuf.at[:, up(lo, n_lo, step), :, :, span(k)]
            copy = remote(
                source, part_one.at[step - 1, pl.ds(0, source.shape[0]), :, :, span(k)],
                one_send.at[k, step - 1], one_recv.at[k, step - 1], at_hi(step) if k % 2 else at_lo(step),
            )
            copy.start()
            copies.append(copy)
        return copies

    def stage_two(k, copies):
        for copy in copies:
            copy.wait_recv()
        for i in range(n_lo if k % 2 else n_hi):
            own = pbuf[hi, i, :, :, span(k)] if k % 2 else pbuf[i, lo, :, :, span(k)]
            total = own.astype(jnp.float32)
            for j in range(len(copies)):
                total = total + part_one[j, i, :, :, span(k)].astype(jnp.float32)
            sum_one[i, :, :, span(k)] = total.astype(jnp.bfloat16)
        started = []
        for step in range(1, n_lo if k % 2 else n_hi):
            to = up(lo, n_lo, step) if k % 2 else up(hi, n_hi, step)
            copy = remote(
                sum_one.at[to, :, :, span(k)], part_two.at[step - 1, :, :, span(k)],
                two_send.at[k, step - 1], two_recv.at[k, step - 1], at_lo(step) if k % 2 else at_hi(step),
            )
            copy.start()
            started.append(copy)
        return started

    def stage_three(k, copies):
        for copy in copies:
            copy.wait_recv()
        total = sum_one[lo if k % 2 else hi, :, :, span(k)].astype(jnp.float32)
        for j in range(len(copies)):
            total = total + part_two[j, :, :, span(k)].astype(jnp.float32)
        sums[:, :, span(k)] = total.astype(jnp.bfloat16)
        started = []
        for step in range(1, n_ctx):
            to = up(c, n_ctx, step)
            copy = remote(
                sums.at[to, :, span(k)], part_c.at[step - 1, :, span(k)],
                b_send.at[k, step - 1], b_recv.at[k, step - 1], (g, to, v),
            )
            copy.start()
            started.append(copy)
        return started

    one, two, b_copies = {}, {}, []
    for k in range(CHUNKS):
        partials(k)
        if k < 4:
            one[k] = stage_one(k)
    for p in range(0, CHUNKS + 2, 2):
        for k in (p, p + 1):
            if k < CHUNKS:
                two[k] = stage_two(k, one[k])
                if k + 4 < CHUNKS:
                    one[k + 4] = stage_one(k + 4)
        for k in (p - 2, p - 1):
            if k >= 0:
                b_copies += stage_three(k, two[k])
    for copies in list(one.values()) + list(two.values()):
        pending += copies
    for k in range(CHUNKS):
        cols = slice(k * chunk, (k + 1) * chunk)
        for step in range(1, n_ctx):
            b_copies[k * (n_ctx - 1) + step - 1].wait_recv()
        total = sums[c, :, cols].astype(jnp.float32)
        for step in range(1, n_ctx):
            total = total + part_c[step - 1, :, cols].astype(jnp.float32)
        rows_out[:, cols] = total.astype(jnp.bfloat16)

    for copy in pending + b_copies:
        copy.wait_send()
    for copy in d_copies:
        copy.wait()
    store_h.wait()
    store_g.wait()


def per_device(
    hidden, head_weight, targets, segment_ids, lengths, loss_mask, advantages, ref_logprobs
):
    n_dp, n_ctx, n_vocab = lax.axis_size("dp"), lax.axis_size("ctx"), lax.axis_size("vocab")
    block, depth = hidden.shape
    width = head_weight.shape[1]
    root = math.isqrt(n_vocab)
    n_lo = root if root * root == n_vocab else n_vocab
    n_hi = n_vocab // n_lo
    wide = max(n_hi, n_lo)
    tokens = block * n_ctx
    out_rows = block // n_vocab
    bf16, f32 = jnp.bfloat16, jnp.float32
    dma = pltpu.SemaphoreType.DMA
    anywhere = pl.BlockSpec(memory_space=pl.ANY)
    smem = pl.BlockSpec(memory_space=pltpu.SMEM)
    vmem = pl.BlockSpec(memory_space=pltpu.VMEM)
    grad_hidden, hid_all, grad_all = pl.pallas_call(
        functools.partial(kernel, n_dp, n_ctx, n_hi, n_lo),
        out_shape=(
            jax.ShapeDtypeStruct((out_rows, depth), bf16),
            jax.ShapeDtypeStruct((n_dp, tokens, depth), bf16),
            jax.ShapeDtypeStruct((n_dp, tokens, width), bf16),
        ),
        in_specs=[anywhere, anywhere, smem, smem, vmem, vmem, vmem, vmem],
        out_specs=(vmem, anywhere, anywhere),
        scratch_shapes=[
            pltpu.VMEM((width, depth), bf16),
            pltpu.VMEM((tokens, depth), bf16),
            pltpu.VMEM((tokens, width), f32),
            pltpu.VMEM((128, tokens), f32),
            pltpu.VMEM((tokens, 128), f32),
            pltpu.VMEM((tokens, 128), f32),
            pltpu.VMEM((tokens, 128), f32),
            pltpu.VMEM((STATS, tokens), f32),
            pltpu.VMEM((STATS, tokens), f32),
            pltpu.VMEM((n_vocab - 1, STATS, tokens), f32),
            pltpu.VMEM((n_ctx - 1, STATS, tokens), f32),
            pltpu.VMEM((tokens, width), bf16),
            pltpu.VMEM((n_hi, n_lo, n_ctx, out_rows, depth), bf16),
            pltpu.VMEM((wide - 1, wide, n_ctx, out_rows, depth), bf16),
            pltpu.VMEM((wide, n_ctx, out_rows, depth), bf16),
            pltpu.VMEM((wide - 1, n_ctx, out_rows, depth), bf16),
            pltpu.VMEM((n_ctx, out_rows, depth), bf16),
            pltpu.VMEM((n_ctx - 1, out_rows, depth), bf16),
            dma((4,)),
            dma((n_ctx - 1,)), dma((n_ctx - 1,)),
            dma((n_ctx - 1, wide, 2)), dma((n_ctx - 1, wide, 2)),
            dma((n_ctx - 1, wide, 2)), dma((n_ctx - 1, wide, 2)),
            dma((n_ctx - 1, wide, wide)), dma((n_ctx - 1, wide, wide)),
            dma((n_ctx - 1, wide, wide)), dma((n_ctx - 1, wide, wide)),
            dma((n_dp - 1,)), dma((n_dp - 1,)), dma((n_dp - 1,)), dma((n_dp - 1,)),
            dma((n_vocab - 1,)), dma((n_vocab - 1,)),
            dma((n_ctx - 1,)), dma((n_ctx - 1,)),
            dma((CHUNKS, wide)), dma((CHUNKS, wide)),
            dma((CHUNKS, wide)), dma((CHUNKS, wide)),
            dma((CHUNKS, n_ctx - 1)), dma((CHUNKS, n_ctx - 1)),
        ],
        compiler_params=pltpu.CompilerParams(collective_id=0, has_side_effects=True),
    )(
        hidden, head_weight.T, lengths, advantages,
        targets[None, :], segment_ids[None, :], loss_mask[None, :], ref_logprobs[None, :],
    )
    grad_head = lax.dot_general(
        grad_all.reshape(n_dp * tokens, width),
        hid_all.reshape(n_dp * tokens, depth),
        (((0,), (0,)), ((), ())),
        preferred_element_type=jnp.float32,
    ).astype(bf16).T
    return (grad_hidden, grad_head)


def solution(mesh):
    return jax.shard_map(
        per_device,
        mesh=mesh,
        in_specs=(
            P(("dp", "ctx"), None),
            P(None, ("ctx", "vocab")),
            P("dp"),
            P("dp"),
            P(),
            P("dp"),
            P(),
            P("dp"),
        ),
        out_specs=(P(("dp", "ctx", "vocab"), None), P(None, ("ctx", "vocab"))),
        check_vma=False,
    )
```

```python
import functools
import math

import jax
import jax.numpy as jnp
from jax import lax
from jax.experimental import pallas as pl
from jax.experimental.pallas import tpu as pltpu
from jax.sharding import PartitionSpec as P

LOSS_SCALE = 1024


kl_weight = 0.1
entropy_weight = 0.05
MESH = pl.DeviceIdType.MESH
CHUNKS = 8
STATS = 8


def combine(parts):
    top = functools.reduce(jnp.maximum, [p[0:1] for p in parts])
    scales = [jnp.exp(p[0:1] - top) for p in parts]
    total = sum(p[1:2] * s for p, s in zip(parts, scales))
    logit = sum(p[2:3] * s for p, s in zip(parts, scales))
    target = sum(p[3:4] for p in parts)
    return top, total, logit, target


def kernel(
    n_dp, n_ctx, n_hi, n_lo,
    hid, head, lengths, advantages, targets, segments, mask, ref_lp,
    rows_out, head_out,
    weight, hbuf, logits, rowbuf, colbuf, tcol, statcol, stat_own, stat_mid, stat_v, stat_c,
    hid_other, g_own, g_other, head_buf, gbuf, pbuf, part_one, sum_one, part_two, sums, part_c,
    local_sem, head_sem, z_send, z_recv, lo_send, lo_recv, hi_send, hi_recv, ra_send, ra_recv, rb_send, rb_recv,
    d_send, d_recv, g_send, g_recv,
    sv_send, sv_recv, sc_send, sc_recv, one_send, one_recv, two_send, two_recv, b_send, b_recv,
):
    g, c, v = lax.axis_index("dp"), lax.axis_index("ctx"), lax.axis_index("vocab")
    n_vocab = n_hi * n_lo
    hi, lo = v // n_lo, lax.rem(v, n_lo)
    block, depth = hid.shape
    tokens, width = logits.shape
    quarter = depth // n_vocab
    chunk = depth // CHUNKS
    out_rows = rows_out.shape[0]

    def up(axis, n, step):
        return lax.rem(axis + step, n)

    def down(axis, n, step):
        return lax.rem(axis + n - step, n)

    def remote(src, dst, send, recv, where):
        copy = pltpu.make_async_remote_copy(
            src_ref=src, dst_ref=dst, send_sem=send, recv_sem=recv,
            device_id=where, device_id_type=MESH,
        )
        return copy

    load_w = pltpu.make_async_copy(head, weight, local_sem.at[0])
    load_w.start()
    own_rows = pl.ds(pl.multiple_of(c * block, block), block)
    load_h = pltpu.make_async_copy(hid, hbuf.at[own_rows], local_sem.at[1])
    load_h.start()

    barrier = pltpu.get_barrier_semaphore()
    for step in range(1, n_ctx):
        pl.semaphore_signal(barrier, inc=1, device_id=(g, up(c, n_ctx, step), v), device_id_type=MESH)
    for step in range(1, n_vocab):
        pl.semaphore_signal(barrier, inc=1, device_id=(g, c, up(v, n_vocab, step)), device_id_type=MESH)
    for step in range(1, n_dp):
        pl.semaphore_signal(barrier, inc=1, device_id=(up(g, n_dp, step), c, v), device_id_type=MESH)
    pl.semaphore_wait(barrier, n_ctx + n_vocab + n_dp - 3)

    own_cols = pl.ds(pl.multiple_of(v * quarter, quarter), quarter)
    pending = []
    z_copies = []
    for step in range(1, n_ctx):
        copy = remote(
            hid.at[:, own_cols], hbuf.at[own_rows, own_cols],
            z_send.at[step - 1], z_recv.at[step - 1], (g, up(c, n_ctx, step), v),
        )
        copy.start()
        z_copies.append(copy)
        pending.append(copy)

    seg = segments[...]
    token_adv = jnp.zeros((1, tokens), jnp.float32)
    token_len = jnp.zeros((1, tokens), jnp.float32)
    for s in range(advantages.shape[0]):
        here = seg == s
        token_adv = jnp.where(here, advantages[s], token_adv)
        token_len = jnp.where(here, lengths[s].astype(jnp.float32), token_len)
    token_weight = LOSS_SCALE * mask[...].astype(jnp.float32) / token_len
    rowbuf[...] = jnp.zeros_like(rowbuf)
    rowbuf[0:1, :] = targets[...].astype(jnp.float32)
    tcol[...] = rowbuf[...].T

    first_column = (c * n_vocab + v) * width
    columns = (first_column + lax.broadcasted_iota(jnp.int32, (block, width), 1)).astype(jnp.float32)
    lane = lax.broadcasted_iota(jnp.int32, (block, 128), 1)

    def do_block(owner):
        rows = pl.ds(pl.multiple_of(owner * block, block), block)
        x = lax.dot_general(
            weight[...], hbuf[rows, :], (((1,), (1,)), ((), ())), preferred_element_type=jnp.float32
        ).T
        logits[rows, :] = x
        top = jnp.max(x, axis=1, keepdims=True)
        e = jnp.exp(x - top)
        total = jnp.sum(e, axis=1, keepdims=True)
        logit = jnp.sum(e * x, axis=1, keepdims=True)
        hit = tcol[rows, 0:1] == columns
        target = jnp.sum(jnp.where(hit, x, 0.0), axis=1, keepdims=True)
        statcol[rows, :] = jnp.where(
            lane == 0, top, jnp.where(lane == 1, total, jnp.where(lane == 2, logit, jnp.where(lane == 3, target, 0.0)))
        )

    load_w.wait()
    load_h.wait()
    do_block(c)

    half = quarter // 2

    def share(owner, column_owner, part):
        rows = pl.ds(pl.multiple_of(owner * block, block), block)
        return hbuf.at[rows, pl.ds(pl.multiple_of(column_owner * quarter + part * half, half), half)]

    def at_lo(step):
        return (g, c, hi * n_lo + up(lo, n_lo, step))

    def at_hi(step):
        return (g, c, up(hi, n_hi, step) * n_lo + lo)

    def move(ref, send, recv, where):
        copy = remote(ref, ref, send, recv, where)
        copy.start()
        pending.append(copy)
        return copy

    lo_copies, hi_copies, relays = {}, {}, {}

    def relay(step):
        owner = down(c, n_ctx, step)
        for hop in range(1, n_lo):
            lo_copies[step - 1, hop - 1, 0].wait_recv()
            source = hi * n_lo + down(lo, n_lo, hop)
            for far in range(1, n_hi):
                at = (step - 1, hop - 1, far - 1)
                relays[(step, 0) + at] = move(share(owner, source, 0), ra_send.at[at], ra_recv.at[at], at_hi(far))
        for hop in range(1, n_hi):
            hi_copies[step - 1, hop - 1, 1].wait_recv()
            source = down(hi, n_hi, hop) * n_lo + lo
            for far in range(1, n_lo):
                at = (step - 1, hop - 1, far - 1)
                relays[(step, 1) + at] = move(share(owner, source, 1), rb_send.at[at], rb_recv.at[at], at_lo(far))

    for step in range(1, n_ctx):
        z_copies[step - 1].wait_recv()
        owner = down(c, n_ctx, step)
        for part in range(2):
            for hop in range(1, n_lo):
                at = (step - 1, hop - 1, part)
                lo_copies[at] = move(share(owner, v, part), lo_send.at[at], lo_recv.at[at], at_lo(hop))
            for hop in range(1, n_hi):
                at = (step - 1, hop - 1, 1 - part)
                hi_copies[at] = move(share(owner, v, 1 - part), hi_send.at[at], hi_recv.at[at], at_hi(hop))
        if step >= 2:
            relay(step - 1)
    relay(n_ctx - 1)
    for step in range(1, n_ctx):
        for copies in (lo_copies, hi_copies):
            for at, copy in copies.items():
                if at[0] == step - 1 and at[2] == (1 if copies is lo_copies else 0):
                    copy.wait_recv()
        for at, copy in relays.items():
            if at[0] == step:
                copy.wait_recv()
        do_block(down(c, n_ctx, step))

    d_copies = []
    for step in range(1, n_dp):
        copy = remote(hbuf, hid_other.at[step - 1], d_send.at[step - 1], d_recv.at[step - 1], (up(g, n_dp, step), c, v))
        copy.start()
        d_copies.append(copy)

    stat_own[...] = statcol[...].T[0:STATS, :]
    s_copies = []
    for step in range(1, n_vocab):
        copy = remote(stat_own, stat_v.at[step - 1], sv_send.at[step - 1], sv_recv.at[step - 1], (g, c, up(v, n_vocab, step)))
        copy.start()
        s_copies.append(copy)
    for copy in s_copies:
        copy.wait_recv()
    pending += s_copies
    merged = combine([stat_own[...]] + [stat_v[i] for i in range(n_vocab - 1)])
    for i, row in enumerate(merged):
        stat_mid[i : i + 1, :] = row
    s_copies = []
    for step in range(1, n_ctx):
        copy = remote(stat_mid, stat_c.at[step - 1], sc_send.at[step - 1], sc_recv.at[step - 1], (g, up(c, n_ctx, step), v))
        copy.start()
        s_copies.append(copy)
    for copy in s_copies:
        copy.wait_recv()
    pending += s_copies
    row_max, exp_total, exp_logit, target_logit = combine([stat_mid[...]] + [stat_c[i] for i in range(n_ctx - 1)])
    log_total = row_max + jnp.log(exp_total)
    rowbuf[0:1, :] = log_total
    rowbuf[1:2, :] = exp_logit / exp_total
    rowbuf[2:3, :] = -token_adv + kl_weight * ((target_logit - log_total) - ref_lp[...])
    rowbuf[3:4, :] = token_weight
    colbuf[...] = rowbuf[...].T

    for b in range(n_ctx):
        rows = slice(b * block, (b + 1) * block)
        x = logits[rows, :]
        probs = jnp.exp(x - colbuf[rows, 0:1])
        hit = (tcol[rows, 0:1] == columns).astype(jnp.float32)
        inner = colbuf[rows, 2:3] * (hit - probs)
        inner = inner + entropy_weight * probs * (x - colbuf[rows, 1:2])
        gbuf[rows, :] = (colbuf[rows, 3:4] * inner).astype(jnp.bfloat16)

    def span(k):
        return pl.ds(k * chunk, chunk)

    def partials(k):
        part = jnp.dot(gbuf[...], weight[:, k * chunk : (k + 1) * chunk], preferred_element_type=jnp.float32)
        for i in range(n_ctx):
            for j in range(n_vocab):
                first = i * block + j * out_rows
                pbuf[j // n_lo, j % n_lo, i, :, span(k)] = part[first : first + out_rows].astype(jnp.bfloat16)

    def stage_one(k):
        copies = []
        for step in range(1, n_hi if k % 2 else n_lo):
            if k % 2:
                source = pbuf.at[up(hi, n_hi, step), :, :, :, span(k)]
            else:
                source = pbuf.at[:, up(lo, n_lo, step), :, :, span(k)]
            copy = remote(
                source, part_one.at[step - 1, pl.ds(0, source.shape[0]), :, :, span(k)],
                one_send.at[k, step - 1], one_recv.at[k, step - 1], at_hi(step) if k % 2 else at_lo(step),
            )
            copy.start()
            copies.append(copy)
        return copies

    def stage_two(k, copies):
        for copy in copies:
            copy.wait_recv()
        for i in range(n_lo if k % 2 else n_hi):
            own = pbuf[hi, i, :, :, span(k)] if k % 2 else pbuf[i, lo, :, :, span(k)]
            total = own.astype(jnp.float32)
            for j in range(len(copies)):
                total = total + part_one[j, i, :, :, span(k)].astype(jnp.float32)
            sum_one[i, :, :, span(k)] = total.astype(jnp.bfloat16)
        started = []
        for step in range(1, n_lo if k % 2 else n_hi):
            to = up(lo, n_lo, step) if k % 2 else up(hi, n_hi, step)
            copy = remote(
                sum_one.at[to, :, :, span(k)], part_two.at[step - 1, :, :, span(k)],
                two_send.at[k, step - 1], two_recv.at[k, step - 1], at_lo(step) if k % 2 else at_hi(step),
            )
            copy.start()
            started.append(copy)
        return started

    def stage_three(k, copies):
        for copy in copies:
            copy.wait_recv()
        total = sum_one[lo if k % 2 else hi, :, :, span(k)].astype(jnp.float32)
        for j in range(len(copies)):
            total = total + part_two[j, :, :, span(k)].astype(jnp.float32)
        sums[:, :, span(k)] = total.astype(jnp.bfloat16)
        started = []
        for step in range(1, n_ctx):
            to = up(c, n_ctx, step)
            copy = remote(
                sums.at[to, :, span(k)], part_c.at[step - 1, :, span(k)],
                b_send.at[k, step - 1], b_recv.at[k, step - 1], (g, to, v),
            )
            copy.start()
            started.append(copy)
        return started

    one, two, b_copies = {}, {}, []
    for k in range(CHUNKS):
        partials(k)
        if k < 4:
            one[k] = stage_one(k)
    g_own[...] = gbuf[...].astype(jnp.float32).T.astype(jnp.bfloat16)
    g_copies = []
    for step in range(1, n_dp):
        copy = remote(g_own, g_other.at[step - 1], g_send.at[step - 1], g_recv.at[step - 1], (up(g, n_dp, step), c, v))
        copy.start()
        g_copies.append(copy)

    def head_chunk(k):
        cols = slice(k * chunk, (k + 1) * chunk)
        total = jnp.dot(g_own[...], hbuf[:, cols], preferred_element_type=jnp.float32)
        for i in range(n_dp - 1):
            total = total + jnp.dot(g_other[i], hid_other[i, :, cols], preferred_element_type=jnp.float32)
        head_buf[:, cols] = total.astype(jnp.bfloat16)
        copy = pltpu.make_async_copy(head_buf.at[:, span(k)], head_out.at[:, span(k)], head_sem.at[k])
        copy.start()
        return copy

    stores = []
    for p in range(0, CHUNKS + 2, 2):
        if p == 2:
            for copy in d_copies + g_copies:
                copy.wait_recv()
        if p >= 2:
            stores += [head_chunk(p - 2), head_chunk(p - 1)]
        for k in (p, p + 1):
            if k < CHUNKS:
                two[k] = stage_two(k, one[k])
                if k + 4 < CHUNKS:
                    one[k + 4] = stage_one(k + 4)
        for k in (p - 2, p - 1):
            if k >= 0:
                b_copies += stage_three(k, two[k])
    for copies in list(one.values()) + list(two.values()):
        pending += copies
    for k in range(CHUNKS):
        cols = slice(k * chunk, (k + 1) * chunk)
        for step in range(1, n_ctx):
            b_copies[k * (n_ctx - 1) + step - 1].wait_recv()
        total = sums[c, :, cols].astype(jnp.float32)
        for step in range(1, n_ctx):
            total = total + part_c[step - 1, :, cols].astype(jnp.float32)
        rows_out[:, cols] = total.astype(jnp.bfloat16)

    for copy in pending + b_copies:
        copy.wait_send()
    for copy in d_copies + g_copies:
        copy.wait_send()
    for copy in stores:
        copy.wait()


def per_device(
    hidden, head_weight, targets, segment_ids, lengths, loss_mask, advantages, ref_logprobs
):
    n_dp, n_ctx, n_vocab = lax.axis_size("dp"), lax.axis_size("ctx"), lax.axis_size("vocab")
    block, depth = hidden.shape
    width = head_weight.shape[1]
    root = math.isqrt(n_vocab)
    n_lo = root if root * root == n_vocab else n_vocab
    n_hi = n_vocab // n_lo
    wide = max(n_hi, n_lo)
    tokens = block * n_ctx
    out_rows = block // n_vocab
    bf16, f32 = jnp.bfloat16, jnp.float32
    dma = pltpu.SemaphoreType.DMA
    anywhere = pl.BlockSpec(memory_space=pl.ANY)
    smem = pl.BlockSpec(memory_space=pltpu.SMEM)
    vmem = pl.BlockSpec(memory_space=pltpu.VMEM)
    grad_hidden, grad_head = pl.pallas_call(
        functools.partial(kernel, n_dp, n_ctx, n_hi, n_lo),
        out_shape=(
            jax.ShapeDtypeStruct((out_rows, depth), bf16),
            jax.ShapeDtypeStruct((width, depth), bf16),
        ),
        in_specs=[anywhere, anywhere, smem, smem, vmem, vmem, vmem, vmem],
        out_specs=(vmem, anywhere),
        scratch_shapes=[
            pltpu.VMEM((width, depth), bf16),
            pltpu.VMEM((tokens, depth), bf16),
            pltpu.VMEM((tokens, width), f32),
            pltpu.VMEM((128, tokens), f32),
            pltpu.VMEM((tokens, 128), f32),
            pltpu.VMEM((tokens, 128), f32),
            pltpu.VMEM((tokens, 128), f32),
            pltpu.VMEM((STATS, tokens), f32),
            pltpu.VMEM((STATS, tokens), f32),
            pltpu.VMEM((n_vocab - 1, STATS, tokens), f32),
            pltpu.VMEM((n_ctx - 1, STATS, tokens), f32),
            pltpu.VMEM((n_dp - 1, tokens, depth), bf16),
            pltpu.VMEM((width, tokens), bf16),
            pltpu.VMEM((n_dp - 1, width, tokens), bf16),
            pltpu.VMEM((width, depth), bf16),
            pltpu.VMEM((tokens, width), bf16),
            pltpu.VMEM((n_hi, n_lo, n_ctx, out_rows, depth), bf16),
            pltpu.VMEM((wide - 1, wide, n_ctx, out_rows, depth), bf16),
            pltpu.VMEM((wide, n_ctx, out_rows, depth), bf16),
            pltpu.VMEM((wide - 1, n_ctx, out_rows, depth), bf16),
            pltpu.VMEM((n_ctx, out_rows, depth), bf16),
            pltpu.VMEM((n_ctx - 1, out_rows, depth), bf16),
            dma((2,)), dma((CHUNKS,)),
            dma((n_ctx - 1,)), dma((n_ctx - 1,)),
            dma((n_ctx - 1, wide, 2)), dma((n_ctx - 1, wide, 2)),
            dma((n_ctx - 1, wide, 2)), dma((n_ctx - 1, wide, 2)),
            dma((n_ctx - 1, wide, wide)), dma((n_ctx - 1, wide, wide)),
            dma((n_ctx - 1, wide, wide)), dma((n_ctx - 1, wide, wide)),
            dma((n_dp - 1,)), dma((n_dp - 1,)), dma((n_dp - 1,)), dma((n_dp - 1,)),
            dma((n_vocab - 1,)), dma((n_vocab - 1,)),
            dma((n_ctx - 1,)), dma((n_ctx - 1,)),
            dma((CHUNKS, wide)), dma((CHUNKS, wide)),
            dma((CHUNKS, wide)), dma((CHUNKS, wide)),
            dma((CHUNKS, n_ctx - 1)), dma((CHUNKS, n_ctx - 1)),
        ],
        compiler_params=pltpu.CompilerParams(collective_id=0, has_side_effects=True),
    )(
        hidden, head_weight.T, lengths, advantages,
        targets[None, :], segment_ids[None, :], loss_mask[None, :], ref_logprobs[None, :],
    )
    return (grad_hidden, grad_head.T)


def solution(mesh):
    return jax.shard_map(
        per_device,
        mesh=mesh,
        in_specs=(
            P(("dp", "ctx"), None),
            P(None, ("ctx", "vocab")),
            P("dp"),
            P("dp"),
            P(),
            P("dp"),
            P(),
            P("dp"),
        ),
        out_specs=(P(("dp", "ctx", "vocab"), None), P(None, ("ctx", "vocab"))),
        check_vma=False,
    )
```

```python
import functools
import math

import jax
import jax.numpy as jnp
from jax import lax
from jax.experimental import pallas as pl
from jax.experimental.pallas import tpu as pltpu
from jax.sharding import PartitionSpec as P

LOSS_SCALE = 1024


kl_weight = 0.1
entropy_weight = 0.05
MESH = pl.DeviceIdType.MESH
CHUNKS = 8
STATS = 8


def combine(parts):
    top = functools.reduce(jnp.maximum, [p[0:1] for p in parts])
    scales = [jnp.exp(p[0:1] - top) for p in parts]
    total = sum(p[1:2] * s for p, s in zip(parts, scales))
    logit = sum(p[2:3] * s for p, s in zip(parts, scales))
    target = sum(p[3:4] for p in parts)
    return top, total, logit, target


def kernel(
    n_dp, n_ctx, n_hi, n_lo,
    hid, head, lengths, advantages, targets, segments, mask, ref_lp,
    rows_out, hid_all, grad_all,
    weight, hbuf, logits, rowbuf, colbuf, tcol, statcol, stat_own, stat_mid, stat_v, stat_c,
    gbuf, pbuf, part_one, sum_one, part_two, sums, part_c,
    local_sem, z_send, z_recv, lo_send, lo_recv, hi_send, hi_recv, ra_send, ra_recv, rb_send, rb_recv,
    d_send, d_recv, g_send, g_recv,
    sv_send, sv_recv, sc_send, sc_recv, one_send, one_recv, two_send, two_recv, b_send, b_recv,
):
    g, c, v = lax.axis_index("dp"), lax.axis_index("ctx"), lax.axis_index("vocab")
    n_vocab = n_hi * n_lo
    hi, lo = v // n_lo, lax.rem(v, n_lo)
    block, depth = hid.shape
    tokens, width = logits.shape
    quarter = depth // n_vocab
    chunk = depth // CHUNKS
    out_rows = rows_out.shape[0]

    def up(axis, n, step):
        return lax.rem(axis + step, n)

    def down(axis, n, step):
        return lax.rem(axis + n - step, n)

    def remote(src, dst, send, recv, where):
        copy = pltpu.make_async_remote_copy(
            src_ref=src, dst_ref=dst, send_sem=send, recv_sem=recv,
            device_id=where, device_id_type=MESH,
        )
        return copy

    load_w = pltpu.make_async_copy(head, weight, local_sem.at[0])
    load_w.start()
    own_rows = pl.ds(pl.multiple_of(c * block, block), block)
    load_h = pltpu.make_async_copy(hid, hbuf.at[own_rows], local_sem.at[1])
    load_h.start()

    barrier = pltpu.get_barrier_semaphore()
    for step in range(1, n_ctx):
        pl.semaphore_signal(barrier, inc=1, device_id=(g, up(c, n_ctx, step), v), device_id_type=MESH)
    for step in range(1, n_vocab):
        pl.semaphore_signal(barrier, inc=1, device_id=(g, c, up(v, n_vocab, step)), device_id_type=MESH)
    for step in range(1, n_dp):
        pl.semaphore_signal(barrier, inc=1, device_id=(up(g, n_dp, step), c, v), device_id_type=MESH)
    pl.semaphore_wait(barrier, n_ctx + n_vocab + n_dp - 3)

    pending = []
    z_copies = {}
    for step in range(1, n_ctx):
        for part in range(2):
            cols = pl.ds(pl.multiple_of(v * quarter + part * (quarter // 2), quarter // 2), quarter // 2)
            copy = remote(
                hid.at[:, cols], hbuf.at[own_rows, cols],
                z_send.at[step - 1, part], z_recv.at[step - 1, part], (g, up(c, n_ctx, step), v),
            )
            copy.start()
            z_copies[step - 1, part] = copy
            pending.append(copy)

    seg = segments[...]
    token_adv = jnp.zeros((1, tokens), jnp.float32)
    token_len = jnp.zeros((1, tokens), jnp.float32)
    for s in range(advantages.shape[0]):
        here = seg == s
        token_adv = jnp.where(here, advantages[s], token_adv)
        token_len = jnp.where(here, lengths[s].astype(jnp.float32), token_len)
    token_weight = LOSS_SCALE * mask[...].astype(jnp.float32) / token_len
    rowbuf[...] = jnp.zeros_like(rowbuf)
    rowbuf[0:1, :] = targets[...].astype(jnp.float32)
    tcol[...] = rowbuf[...].T

    first_column = (c * n_vocab + v) * width
    columns = (first_column + lax.broadcasted_iota(jnp.int32, (block, width), 1)).astype(jnp.float32)
    lane = lax.broadcasted_iota(jnp.int32, (block, 128), 1)

    def do_block(owner):
        rows = pl.ds(pl.multiple_of(owner * block, block), block)
        x = lax.dot_general(
            weight[...], hbuf[rows, :], (((1,), (1,)), ((), ())), preferred_element_type=jnp.float32
        ).T
        logits[rows, :] = x
        top = jnp.max(x, axis=1, keepdims=True)
        e = jnp.exp(x - top)
        total = jnp.sum(e, axis=1, keepdims=True)
        logit = jnp.sum(e * x, axis=1, keepdims=True)
        hit = tcol[rows, 0:1] == columns
        target = jnp.sum(jnp.where(hit, x, 0.0), axis=1, keepdims=True)
        statcol[rows, :] = jnp.where(
            lane == 0, top, jnp.where(lane == 1, total, jnp.where(lane == 2, logit, jnp.where(lane == 3, target, 0.0)))
        )

    load_w.wait()
    load_h.wait()
    do_block(c)

    half = quarter // 2

    def share(owner, column_owner, part):
        rows = pl.ds(pl.multiple_of(owner * block, block), block)
        return hbuf.at[rows, pl.ds(pl.multiple_of(column_owner * quarter + part * half, half), half)]

    def at_lo(step):
        return (g, c, hi * n_lo + up(lo, n_lo, step))

    def at_hi(step):
        return (g, c, up(hi, n_hi, step) * n_lo + lo)

    def move(ref, send, recv, where):
        copy = remote(ref, ref, send, recv, where)
        copy.start()
        pending.append(copy)
        return copy

    lo_copies, hi_copies, relays = {}, {}, {}

    def relay(step):
        owner = down(c, n_ctx, step)
        for hop in range(1, n_lo):
            lo_copies[step - 1, hop - 1, 0].wait_recv()
            source = hi * n_lo + down(lo, n_lo, hop)
            for far in range(1, n_hi):
                at = (step - 1, hop - 1, far - 1)
                relays[(step, 0) + at] = move(share(owner, source, 0), ra_send.at[at], ra_recv.at[at], at_hi(far))
        for hop in range(1, n_hi):
            hi_copies[step - 1, hop - 1, 1].wait_recv()
            source = down(hi, n_hi, hop) * n_lo + lo
            for far in range(1, n_lo):
                at = (step - 1, hop - 1, far - 1)
                relays[(step, 1) + at] = move(share(owner, source, 1), rb_send.at[at], rb_recv.at[at], at_lo(far))

    def finish(step):
        for copies in (lo_copies, hi_copies):
            for at, copy in copies.items():
                if at[0] == step - 1 and at[2] == (1 if copies is lo_copies else 0):
                    copy.wait_recv()
        for at, copy in relays.items():
            if at[0] == step:
                copy.wait_recv()
        do_block(down(c, n_ctx, step))

    for step in range(1, n_ctx):
        owner = down(c, n_ctx, step)
        for part in range(2):
            z_copies[step - 1, part].wait_recv()
            for hop in range(1, n_lo):
                at = (step - 1, hop - 1, part)
                lo_copies[at] = move(share(owner, v, part), lo_send.at[at], lo_recv.at[at], at_lo(hop))
            for hop in range(1, n_hi):
                at = (step - 1, hop - 1, part)
                hi_copies[at] = move(share(owner, v, part), hi_send.at[at], hi_recv.at[at], at_hi(hop))
        if step >= 2:
            relay(step - 1)
        if step >= 3:
            finish(step - 2)
    relay(n_ctx - 1)
    for step in range(max(1, n_ctx - 2), n_ctx):
        finish(step)

    store_h = pltpu.make_async_copy(hbuf, hid_all.at[g], local_sem.at[2])
    store_h.start()
    d_copies = []
    for step in range(1, n_dp):
        copy = remote(hbuf, hid_all.at[g], d_send.at[step - 1], d_recv.at[step - 1], (up(g, n_dp, step), c, v))
        copy.start()
        d_copies.append(copy)

    stat_own[...] = statcol[...].T[0:STATS, :]
    s_copies = []
    for step in range(1, n_vocab):
        copy = remote(stat_own, stat_v.at[step - 1], sv_send.at[step - 1], sv_recv.at[step - 1], (g, c, up(v, n_vocab, step)))
        copy.start()
        s_copies.append(copy)
    for copy in s_copies:
        copy.wait_recv()
    pending += s_copies
    merged = combine([stat_own[...]] + [stat_v[i] for i in range(n_vocab - 1)])
    for i, row in enumerate(merged):
        stat_mid[i : i + 1, :] = row
    s_copies = []
    for step in range(1, n_ctx):
        copy = remote(stat_mid, stat_c.at[step - 1], sc_send.at[step - 1], sc_recv.at[step - 1], (g, up(c, n_ctx, step), v))
        copy.start()
        s_copies.append(copy)
    for copy in s_copies:
        copy.wait_recv()
    pending += s_copies
    row_max, exp_total, exp_logit, target_logit = combine([stat_mid[...]] + [stat_c[i] for i in range(n_ctx - 1)])
    log_total = row_max + jnp.log(exp_total)
    rowbuf[0:1, :] = log_total
    rowbuf[1:2, :] = exp_logit / exp_total
    rowbuf[2:3, :] = -token_adv + kl_weight * ((target_logit - log_total) - ref_lp[...])
    rowbuf[3:4, :] = token_weight
    colbuf[...] = rowbuf[...].T

    for b in range(n_ctx):
        rows = slice(b * block, (b + 1) * block)
        x = logits[rows, :]
        probs = jnp.exp(x - colbuf[rows, 0:1])
        hit = (tcol[rows, 0:1] == columns).astype(jnp.float32)
        inner = colbuf[rows, 2:3] * (hit - probs)
        inner = inner + entropy_weight * probs * (x - colbuf[rows, 1:2])
        gbuf[rows, :] = (colbuf[rows, 3:4] * inner).astype(jnp.bfloat16)

    store_g = pltpu.make_async_copy(gbuf, grad_all.at[g], local_sem.at[3])
    store_g.start()
    for step in range(1, n_dp):
        copy = remote(gbuf, grad_all.at[g], g_send.at[step - 1], g_recv.at[step - 1], (up(g, n_dp, step), c, v))
        copy.start()
        d_copies.append(copy)

    def span(k):
        return pl.ds(k * chunk, chunk)

    def partials(k):
        part = jnp.dot(gbuf[...], weight[:, k * chunk : (k + 1) * chunk], preferred_element_type=jnp.float32)
        for i in range(n_ctx):
            for j in range(n_vocab):
                first = i * block + j * out_rows
                pbuf[j // n_lo, j % n_lo, i, :, span(k)] = part[first : first + out_rows].astype(jnp.bfloat16)

    def stage_one(k):
        copies = []
        for step in range(1, n_hi if k % 2 else n_lo):
            if k % 2:
                source = pbuf.at[up(hi, n_hi, step), :, :, :, span(k)]
            else:
                source = pbuf.at[:, up(lo, n_lo, step), :, :, span(k)]
            copy = remote(
                source, part_one.at[step - 1, pl.ds(0, source.shape[0]), :, :, span(k)],
                one_send.at[k, step - 1], one_recv.at[k, step - 1], at_hi(step) if k % 2 else at_lo(step),
            )
            copy.start()
            copies.append(copy)
        return copies

    def stage_two(k, copies):
        for copy in copies:
            copy.wait_recv()
        for i in range(n_lo if k % 2 else n_hi):
            own = pbuf[hi, i, :, :, span(k)] if k % 2 else pbuf[i, lo, :, :, span(k)]
            total = own.astype(jnp.float32)
            for j in range(len(copies)):
                total = total + part_one[j, i, :, :, span(k)].astype(jnp.float32)
            sum_one[i, :, :, span(k)] = total.astype(jnp.bfloat16)
        started = []
        for step in range(1, n_lo if k % 2 else n_hi):
            to = up(lo, n_lo, step) if k % 2 else up(hi, n_hi, step)
            copy = remote(
                sum_one.at[to, :, :, span(k)], part_two.at[step - 1, :, :, span(k)],
                two_send.at[k, step - 1], two_recv.at[k, step - 1], at_lo(step) if k % 2 else at_hi(step),
            )
            copy.start()
            started.append(copy)
        return started

    def stage_three(k, copies):
        for copy in copies:
            copy.wait_recv()
        total = sum_one[lo if k % 2 else hi, :, :, span(k)].astype(jnp.float32)
        for j in range(len(copies)):
            total = total + part_two[j, :, :, span(k)].astype(jnp.float32)
        sums[:, :, span(k)] = total.astype(jnp.bfloat16)
        started = []
        for step in range(1, n_ctx):
            to = up(c, n_ctx, step)
            copy = remote(
                sums.at[to, :, span(k)], part_c.at[step - 1, :, span(k)],
                b_send.at[k, step - 1], b_recv.at[k, step - 1], (g, to, v),
            )
            copy.start()
            started.append(copy)
        return started

    one, two, b_copies = {}, {}, []
    for k in range(CHUNKS):
        partials(k)
        if k < 4:
            one[k] = stage_one(k)
    for p in range(0, CHUNKS + 2, 2):
        for k in (p, p + 1):
            if k < CHUNKS:
                two[k] = stage_two(k, one[k])
                if k + 4 < CHUNKS:
                    one[k + 4] = stage_one(k + 4)
        for k in (p - 2, p - 1):
            if k >= 0:
                b_copies += stage_three(k, two[k])
    for copies in list(one.values()) + list(two.values()):
        pending += copies
    for k in range(CHUNKS):
        cols = slice(k * chunk, (k + 1) * chunk)
        for step in range(1, n_ctx):
            b_copies[k * (n_ctx - 1) + step - 1].wait_recv()
        total = sums[c, :, cols].astype(jnp.float32)
        for step in range(1, n_ctx):
            total = total + part_c[step - 1, :, cols].astype(jnp.float32)
        rows_out[:, cols] = total.astype(jnp.bfloat16)

    for copy in pending + b_copies:
        copy.wait_send()
    for copy in d_copies:
        copy.wait()
    store_h.wait()
    store_g.wait()


def per_device(
    hidden, head_weight, targets, segment_ids, lengths, loss_mask, advantages, ref_logprobs
):
    n_dp, n_ctx, n_vocab = lax.axis_size("dp"), lax.axis_size("ctx"), lax.axis_size("vocab")
    block, depth = hidden.shape
    width = head_weight.shape[1]
    root = math.isqrt(n_vocab)
    n_lo = root if root * root == n_vocab else n_vocab
    n_hi = n_vocab // n_lo
    wide = max(n_hi, n_lo)
    tokens = block * n_ctx
    out_rows = block // n_vocab
    bf16, f32 = jnp.bfloat16, jnp.float32
    dma = pltpu.SemaphoreType.DMA
    anywhere = pl.BlockSpec(memory_space=pl.ANY)
    smem = pl.BlockSpec(memory_space=pltpu.SMEM)
    vmem = pl.BlockSpec(memory_space=pltpu.VMEM)
    grad_hidden, hid_all, grad_all = pl.pallas_call(
        functools.partial(kernel, n_dp, n_ctx, n_hi, n_lo),
        out_shape=(
            jax.ShapeDtypeStruct((out_rows, depth), bf16),
            jax.ShapeDtypeStruct((n_dp, tokens, depth), bf16),
            jax.ShapeDtypeStruct((n_dp, tokens, width), bf16),
        ),
        in_specs=[anywhere, anywhere, smem, smem, vmem, vmem, vmem, vmem],
        out_specs=(vmem, anywhere, anywhere),
        scratch_shapes=[
            pltpu.VMEM((width, depth), bf16),
            pltpu.VMEM((tokens, depth), bf16),
            pltpu.VMEM((tokens, width), f32),
            pltpu.VMEM((128, tokens), f32),
            pltpu.VMEM((tokens, 128), f32),
            pltpu.VMEM((tokens, 128), f32),
            pltpu.VMEM((tokens, 128), f32),
            pltpu.VMEM((STATS, tokens), f32),
            pltpu.VMEM((STATS, tokens), f32),
            pltpu.VMEM((n_vocab - 1, STATS, tokens), f32),
            pltpu.VMEM((n_ctx - 1, STATS, tokens), f32),
            pltpu.VMEM((tokens, width), bf16),
            pltpu.VMEM((n_hi, n_lo, n_ctx, out_rows, depth), bf16),
            pltpu.VMEM((wide - 1, wide, n_ctx, out_rows, depth), bf16),
            pltpu.VMEM((wide, n_ctx, out_rows, depth), bf16),
            pltpu.VMEM((wide - 1, n_ctx, out_rows, depth), bf16),
            pltpu.VMEM((n_ctx, out_rows, depth), bf16),
            pltpu.VMEM((n_ctx - 1, out_rows, depth), bf16),
            dma((4,)),
            dma((n_ctx - 1, 2)), dma((n_ctx - 1, 2)),
            dma((n_ctx - 1, wide, 2)), dma((n_ctx - 1, wide, 2)),
            dma((n_ctx - 1, wide, 2)), dma((n_ctx - 1, wide, 2)),
            dma((n_ctx - 1, wide, wide)), dma((n_ctx - 1, wide, wide)),
            dma((n_ctx - 1, wide, wide)), dma((n_ctx - 1, wide, wide)),
            dma((n_dp - 1,)), dma((n_dp - 1,)), dma((n_dp - 1,)), dma((n_dp - 1,)),
            dma((n_vocab - 1,)), dma((n_vocab - 1,)),
            dma((n_ctx - 1,)), dma((n_ctx - 1,)),
            dma((CHUNKS, wide)), dma((CHUNKS, wide)),
            dma((CHUNKS, wide)), dma((CHUNKS, wide)),
            dma((CHUNKS, n_ctx - 1)), dma((CHUNKS, n_ctx - 1)),
        ],
        compiler_params=pltpu.CompilerParams(collective_id=0, has_side_effects=True),
    )(
        hidden, head_weight.T, lengths, advantages,
        targets[None, :], segment_ids[None, :], loss_mask[None, :], ref_logprobs[None, :],
    )
    grad_head = lax.dot_general(
        grad_all.reshape(n_dp * tokens, width),
        hid_all.reshape(n_dp * tokens, depth),
        (((0,), (0,)), ((), ())),
        preferred_element_type=jnp.float32,
    ).astype(bf16).T
    return (grad_hidden, grad_head)


def solution(mesh):
    return jax.shard_map(
        per_device,
        mesh=mesh,
        in_specs=(
            P(("dp", "ctx"), None),
            P(None, ("ctx", "vocab")),
            P("dp"),
            P("dp"),
            P(),
            P("dp"),
            P(),
            P("dp"),
        ),
        out_specs=(P(("dp", "ctx", "vocab"), None), P(None, ("ctx", "vocab"))),
        check_vma=False,
    )
```
